32 devices in a mesh: seq: 8 (over z, core), tp: 4 (over y, x).
Axes of the slice: x: 2, y: 2, z: 4, core: 2. Of those that a mesh axis runs over, the one named last changes fastest.
Arguments:
- tokens: bfloat16 [64, 6144], P('seq'), may hold values from -6 to 6
- out_grad: bfloat16 [64, 6144], P('seq'), may hold values from -1.5 to 1.5
- w_in: bfloat16 [6144, 24576], P('seq', 'tp'), may hold values from -0.078125 to 0.078125
- w_out: bfloat16 [24576, 6144], P('tp', 'seq'), may hold values from -0.0390625 to 0.0390625
Outputs:
- input_grad: bfloat16 [64, 6144], P('tp', 'seq')
- grad_in: float32 [6144, 24576], P('seq', 'tp')
- grad_out: float32 [24576, 6144], P('tp', 'seq')
The draws below stay inside these ranges and needn't reach their ends.
All inputs are finite; a program needn't handle non-finite values.
Results may differ from the reference program's by a relative error of at most 0.0051.
Values may be sent and summed in bfloat16 or wider, within the bound.
A program may use at most 128 MiB of HBM per device.

```python
import jax
import jax.numpy as jnp

D = 6144
FF = 24576
TOKENS = 64


def block_levels(key, dims, pieces, smallest, high):
    def one(dim, parts):
        draws = jax.random.uniform(jax.random.fold_in(jax.random.fold_in(key, 6), dim), (parts,), jnp.float32, smallest / len(pieces), high / len(pieces))
        return jnp.repeat(jnp.exp(draws), dims[dim] // parts).reshape((-1,) + (1,) * (len(dims) - dim - 1))

    gain = one(*pieces[0])
    for cut in pieces[1:]:
        gain = gain * one(*cut)
    return gain


def noise(own_key, dims, width, limit, cuts=(), dtype=jnp.bfloat16):
    gain = block_levels(own_key, dims, cuts, -0.22, 0.18) if cuts else 1.0
    drawn = jax.random.normal(own_key, dims, jnp.float32) * width * gain
    return jnp.minimum(jnp.maximum(drawn, -limit), limit).astype(dtype)


def setup_inputs(seed: int = 0) -> dict:
    key_list = jax.random.split(jax.random.key(seed), 5)
    return {
        "tokens": noise(key_list[0], (TOKENS, D), 1.0, 6.0, ((0, 8),)),
        "out_grad": noise(key_list[1], (TOKENS, D), 0.25, 1.5, ((0, 8),)),
        "w_in": noise(key_list[2], (D, FF), D ** -0.5, 0.078125, ((0, 8), (1, 4))),
        "w_out": noise(key_list[3], (FF, D), FF ** -0.5, 0.0390625, ((0, 4), (1, 8))),
    }


def reference(tokens, out_grad, w_in, w_out):
    pre = jnp.dot(tokens, w_in, preferred_element_type=jnp.float32)
    posit = jnp.maximum(pre, 0.0)
    act = (posit * posit).astype(jnp.bfloat16)
    hidden_grad = jnp.dot(out_grad, w_out.T, preferred_element_type=jnp.float32)
    slope = (2.0 * posit * hidden_grad).astype(jnp.bfloat16)
    grad_out = jnp.dot(act.T, out_grad, preferred_element_type=jnp.float32)
    grad_in = jnp.dot(tokens.T, slope, preferred_element_type=jnp.float32)
    input_grad = jnp.dot(slope, w_in.T, preferred_element_type=jnp.float32).astype(jnp.bfloat16)
    return input_grad, grad_in, grad_out
```

```python
import functools

import jax
import jax.numpy as jnp
from jax import lax
from jax.experimental import pallas as pl
from jax.experimental.pallas import tpu as pltpu
from jax.sharding import PartitionSpec as P

CHUNKS = 12
LAG = 2
F32 = jnp.float32
BF16 = jnp.bfloat16


def remote(src, dst, send_sem, recv_sem, axis, target):
    return pltpu.make_async_remote_copy(
        src_ref=src,
        dst_ref=dst,
        send_sem=send_sem,
        recv_sem=recv_sem,
        device_id={axis: target},
        device_id_type=pl.DeviceIdType.MESH,
    )


def loop(lo, hi, body):
    lax.fori_loop(lo, hi, lambda i, carry: (body(i), carry)[1], 0)


def hidden_kernel(
    n_seq, n_tp,
    tokens, out_grad, w_in, w_out,
    hidden_out, cols_out, input_grad,
    w_in_v, w_out_v, cols_in, cols, own,
    core_out, core_got, right_out, left_got, left_out, right_got,
    hidden, total, tp_got,
    w_sem, a2a_send, a2a_recv, core_send, core_recv,
    right_send, right_recv, left_send, left_recv,
    hid_send, hid_recv, tp_send, tp_recv, out_sem,
):
    seq, tp = lax.axis_index("seq"), lax.axis_index("tp")
    n_tok = cols.shape[1]
    feats = cols.shape[2]
    half = n_tok // 2
    wide = w_in_v.shape[2]
    n = CHUNKS
    chip, core = seq // 2, seq % 2
    last = n_seq // 2 - 1
    partner = chip * 2 + 1 - core
    right_dev = lax.rem(seq + 2, n_seq)
    left_dev = lax.rem(seq + n_seq - 2, n_seq)

    def w_copies(c):
        at = pl.ds(pl.multiple_of(c * wide, wide), wide)
        return (
            pltpu.make_async_copy(w_in.at[:, at], w_in_v.at[c], w_sem.at[0, c]),
            pltpu.make_async_copy(w_out.at[at, :], w_out_v.at[c], w_sem.at[1, c]),
        )

    def start_weights(c):
        for copy in w_copies(c):
            copy.start()

    loop(0, n, start_weights)

    barrier = pltpu.get_barrier_semaphore()

    def greet_seq(o):
        pl.semaphore_signal(barrier, inc=1, device_id={"seq": lax.rem(seq + o, n_seq)},
                            device_id_type=pl.DeviceIdType.MESH)

    def greet_tp(o):
        pl.semaphore_signal(barrier, inc=1, device_id={"tp": lax.rem(tp + o, n_tp)},
                            device_id_type=pl.DeviceIdType.MESH)

    loop(1, n_seq, greet_seq)
    loop(1, n_tp, greet_tp)
    pl.semaphore_wait(barrier, n_seq + n_tp - 2)

    def a2a(a, o):
        peer = lax.rem(seq + o, n_seq)
        src = (tokens, out_grad)[a]
        at = pl.ds(pl.multiple_of(peer * feats, feats), feats)
        return remote(src.at[:, at], cols_in.at[a, seq], a2a_send.at[a, peer],
                      a2a_recv.at[a, seq], "seq", peer)

    def a2a_arrival(a, o):
        peer = lax.rem(seq + o, n_seq)
        src = (tokens, out_grad)[a]
        at = pl.ds(pl.multiple_of(peer * feats, feats), feats)
        return remote(src.at[:, at], cols_in.at[a, peer], a2a_send.at[a, peer],
                      a2a_recv.at[a, peer], "seq", peer)

    def start_a2a(o):
        for a in range(2):
            a2a(a, o).start()

    loop(1, n_seq, start_a2a)
    mine = pl.ds(pl.multiple_of(seq * feats, feats), feats)
    cols_in[0, seq] = tokens[:, mine]
    cols_in[1, seq] = out_grad[:, mine]
    total[...] = jnp.zeros_like(total)

    @pl.when(chip == 0)
    def _():
        left_got[...] = jnp.zeros_like(left_got)

    @pl.when(chip == last)
    def _():
        right_got[...] = jnp.zeros_like(right_got)

    def wait_a2a(o):
        for a in range(2):
            a2a_arrival(a, o).wait_recv()

    loop(1, n_seq, wait_a2a)
    for a in range(2):
        cols[a] = cols_in[a].astype(F32).reshape(n_tok, feats).astype(BF16)

    def core_copy(c):
        return remote(core_out.at[c], core_got.at[c], core_send.at[c],
                      core_recv.at[c], "seq", partner)

    def right_copy(c):
        return remote(right_out.at[c], left_got.at[c], right_send.at[c],
                      right_recv.at[c], "seq", right_dev)

    def left_copy(c):
        return remote(left_out.at[c], right_got.at[c], left_send.at[c],
                      left_recv.at[c], "seq", left_dev)

    def hid_copy(c, which):
        part = hidden.at[c, which]
        return remote(part, part, hid_send.at[c], hid_recv.at[c], "seq", partner)

    def step(i):
        @pl.when(i < n)
        def _():
            for copy in w_copies(i):
                copy.wait()
            pre = jnp.dot(cols[0], w_in_v[i], preferred_element_type=F32)
            grad = lax.dot_general(cols[1], w_out_v[i], (((1,), (1,)), ((), ())),
                                   preferred_element_type=F32)
            for a, value in enumerate((pre, grad)):
                low, high = value[:half], value[half:]
                own[i, a] = jnp.where(core == 0, low, high)
                core_out[i, a] = jnp.where(core == 0, high, low).astype(BF16)
            core_copy(i).start()

        near = i - 1

        @pl.when((near >= 0) & (near < n))
        def _():
            core_copy(near).wait_recv()
            own[near] = own[near] + core_got[near].astype(F32)

        from_left = i - 1 - chip * LAG

        @pl.when((from_left >= 0) & (from_left < n))
        def _():
            @pl.when(chip > 0)
            def _():
                right_copy(from_left).wait_recv()

            @pl.when(chip < last)
            def _():
                right_out[from_left] = (
                    left_got[from_left].astype(F32) + own[from_left]
                ).astype(BF16)
                right_copy(from_left).start()

        from_right = i - 1 - (last - chip) * LAG

        @pl.when((from_right >= 0) & (from_right < n))
        def _():
            @pl.when(chip < last)
            def _():
                left_copy(from_right).wait_recv()

            @pl.when(chip > 0)
            def _():
                left_out[from_right] = (
                    right_got[from_right].astype(F32) + own[from_right]
                ).astype(BF16)
                left_copy(from_right).start()

        done = i - 1 - jnp.maximum(chip, last - chip) * LAG

        @pl.when((done >= 0) & (done < n))
        def _():
            value = own[done] + left_got[done].astype(F32) + right_got[done].astype(F32)
            posit = jnp.maximum(value[0], 0.0)
            hidden[done, core, 0] = (posit * posit).astype(BF16)
            hidden[done, core, 1] = (2.0 * posit * value[1]).astype(BF16)
            hid_copy(done, core).start()

        both = done - 1

        @pl.when((both >= 0) & (both < n))
        def _():
            hid_copy(both, 1 - core).wait_recv()
            slope = jnp.concatenate([hidden[both, 0, 1], hidden[both, 1, 1]], axis=0)
            part = lax.dot_general(slope, w_in_v[both], (((1,), (1,)), ((), ())),
                                   preferred_element_type=F32)
            total[...] += part.reshape(total.shape)

    loop(0, n + 2 + last * LAG, step)

    def tp_copy(o):
        peer = lax.rem(tp + o, n_tp)
        return remote(total.at[peer], tp_got.at[tp], tp_send.at[peer],
                      tp_recv.at[tp], "tp", peer)

    def tp_arrival(o):
        peer = lax.rem(tp + o, n_tp)
        return remote(total.at[peer], tp_got.at[peer], tp_send.at[peer],
                      tp_recv.at[peer], "tp", peer)

    loop(1, n_tp, lambda o: tp_copy(o).start())
    outs = (
        pltpu.make_async_copy(hidden, hidden_out, out_sem.at[0]),
        pltpu.make_async_copy(cols, cols_out, out_sem.at[1]),
    )
    for copy in outs:
        copy.start()

    def wait_sends(c):
        core_copy(c).wait_send()
        hid_copy(c, core).wait_send()

        @pl.when(chip < last)
        def _():
            right_copy(c).wait_send()

        @pl.when(chip > 0)
        def _():
            left_copy(c).wait_send()

    loop(0, n, wait_sends)

    def wait_a2a_sends(o):
        for a in range(2):
            a2a(a, o).wait_send()

    loop(1, n_seq, wait_a2a_sends)
    loop(1, n_tp, lambda o: tp_arrival(o).wait_recv())
    tp_got[tp] = total[tp]
    input_grad[...] = jnp.sum(tp_got[...], axis=0).astype(BF16)
    loop(1, n_tp, lambda o: tp_copy(o).wait_send())
    for copy in outs:
        copy.wait()


def grads_kernel(hidden, cols, grad_in, grad_out):
    act = jnp.concatenate([hidden[0, 0, 0], hidden[0, 1, 0]], axis=0)
    slope = jnp.concatenate([hidden[0, 0, 1], hidden[0, 1, 1]], axis=0)
    rows = (((0,), (0,)), ((), ()))
    grad_in[...] = lax.dot_general(cols[0], slope, rows, preferred_element_type=F32)
    grad_out[...] = lax.dot_general(act, cols[1], rows, preferred_element_type=F32)


def per_device(n_seq, n_tp, tokens, out_grad, w_in, w_out):
    n_tok = tokens.shape[0] * n_seq
    feats, units = w_in.shape
    wide = units // CHUNKS
    half = n_tok // 2
    n = CHUNKS
    vmem = pl.BlockSpec(memory_space=pltpu.VMEM)
    hbm = pl.BlockSpec(memory_space=pl.ANY)
    dma = pltpu.SemaphoreType.DMA
    pair = (n, 2, half, wide)
    hidden, cols, input_grad = pl.pallas_call(
        functools.partial(hidden_kernel, n_seq, n_tp),
        out_shape=(
            jax.ShapeDtypeStruct((n, 2, 2, half, wide), BF16),
            jax.ShapeDtypeStruct((2, n_tok, feats), BF16),
            jax.ShapeDtypeStruct((n_tok // n_tp, feats), BF16),
        ),
        in_specs=[vmem, vmem, hbm, hbm],
        out_specs=(hbm, hbm, vmem),
        scratch_shapes=[
            pltpu.VMEM((n, feats, wide), BF16),
            pltpu.VMEM((n, wide, feats), BF16),
            pltpu.VMEM((2, n_seq, tokens.shape[0], feats), BF16),
            pltpu.VMEM((2, n_tok, feats), BF16),
            pltpu.VMEM(pair, F32),
            pltpu.VMEM(pair, BF16),
            pltpu.VMEM(pair, BF16),
            pltpu.VMEM(pair, BF16),
            pltpu.VMEM(pair, BF16),
            pltpu.VMEM(pair, BF16),
            pltpu.VMEM(pair, BF16),
            pltpu.VMEM((n, 2, 2, half, wide), BF16),
            pltpu.VMEM((n_tp, n_tok // n_tp, feats), F32),
            pltpu.VMEM((n_tp, n_tok // n_tp, feats), F32),
            dma((2, n)),
            dma((2, n_seq)),
            dma((2, n_seq)),
            dma((n,)),
            dma((n,)),
            dma((n,)),
            dma((n,)),
            dma((n,)),
            dma((n,)),
            dma((n,)),
            dma((n,)),
            dma((n_tp,)),
            dma((n_tp,)),
            dma((2,)),
        ],
        compiler_params=pltpu.CompilerParams(
            collective_id=0, has_side_effects=True, vmem_limit_bytes=56 * 1024 * 1024
        ),
        name="hidden_exchange",
    )(tokens, out_grad, w_in, w_out)

    grad_in, grad_out = pl.pallas_call(
        grads_kernel,
        grid=(n,),
        out_shape=(
            jax.ShapeDtypeStruct((feats, units), F32),
            jax.ShapeDtypeStruct((units, feats), F32),
        ),
        in_specs=[
            pl.BlockSpec((1, 2, 2, half, wide), lambda c: (c, 0, 0, 0, 0)),
            pl.BlockSpec((2, n_tok, feats), lambda c: (0, 0, 0)),
        ],
        out_specs=(
            pl.BlockSpec((feats, wide), lambda c: (0, c)),
            pl.BlockSpec((wide, feats), lambda c: (c, 0)),
        ),
        name="weight_grads",
    )(hidden, cols)
    return input_grad, grad_in, grad_out


def solution(mesh):
    return jax.shard_map(
        functools.partial(per_device, mesh.shape["seq"], mesh.shape["tp"]),
        mesh=mesh,
        in_specs=(P("seq", None), P("seq", None), P("seq", "tp"), P("tp", "seq")),
        out_specs=(P("tp", "seq"), P("seq", "tp"), P("tp", "seq")),
        check_vma=False,
    )
```

```python
import functools

import jax
import jax.numpy as jnp
from jax import lax
from jax.experimental import pallas as pl
from jax.experimental.pallas import tpu as pltpu
from jax.sharding import PartitionSpec as P

MOST_CHUNKS = 24
LAG = 5
CORE_LAG = 3
HID_LAG = 3
F32 = jnp.float32
BF16 = jnp.bfloat16


def remote(src, dst, send_sem, recv_sem, axis, target):
    return pltpu.make_async_remote_copy(
        src_ref=src,
        dst_ref=dst,
        send_sem=send_sem,
        recv_sem=recv_sem,
        device_id={axis: target},
        device_id_type=pl.DeviceIdType.MESH,
    )


def loop(lo, hi, body):
    lax.fori_loop(lo, hi, lambda i, carry: (body(i), carry)[1], 0)


def hidden_kernel(
    n_seq, n_tp,
    tokens, out_grad, w_in, w_out,
    hidden_out, cols_out, input_grad,
    w_in_v, w_out_v, cols_in, cols, own,
    core_out, core_got, right_out, left_got, left_out, right_got,
    hidden, total, tp_got,
    w_sem, a2a_send, a2a_recv, core_send, core_recv,
    right_send, right_recv, left_send, left_recv,
    hid_send, hid_recv, tp_send, tp_recv, out_sem,
):
    seq, tp = lax.axis_index("seq"), lax.axis_index("tp")
    n_tok = cols.shape[1]
    feats = cols.shape[2]
    half = n_tok // 2
    wide = w_in_v.shape[2]
    n = w_in_v.shape[0]
    chip, core = seq // 2, seq % 2
    last = n_seq // 2 - 1
    partner = chip * 2 + 1 - core
    right_dev = lax.rem(seq + 2, n_seq)
    left_dev = lax.rem(seq + n_seq - 2, n_seq)

    def w_copies(c):
        at = pl.ds(pl.multiple_of(c * wide, wide), wide)
        return (
            pltpu.make_async_copy(w_in.at[:, at], w_in_v.at[c], w_sem.at[0, c]),
            pltpu.make_async_copy(w_out.at[at, :], w_out_v.at[c], w_sem.at[1, c]),
        )

    def start_weights(c):
        for copy in w_copies(c):
            copy.start()

    loop(0, n, start_weights)

    barrier = pltpu.get_barrier_semaphore()

    def greet_seq(o):
        pl.semaphore_signal(barrier, inc=1, device_id={"seq": lax.rem(seq + o, n_seq)},
                            device_id_type=pl.DeviceIdType.MESH)

    def greet_tp(o):
        pl.semaphore_signal(barrier, inc=1, device_id={"tp": lax.rem(tp + o, n_tp)},
                            device_id_type=pl.DeviceIdType.MESH)

    loop(1, n_seq, greet_seq)
    loop(1, n_tp, greet_tp)
    pl.semaphore_wait(barrier, n_seq + n_tp - 2)

    def a2a(a, o):
        peer = lax.rem(seq + o, n_seq)
        src = (tokens, out_grad)[a]
        at = pl.ds(pl.multiple_of(peer * feats, feats), feats)
        return remote(src.at[:, at], cols_in.at[a, seq], a2a_send.at[a, peer],
                      a2a_recv.at[a, seq], "seq", peer)

    def a2a_arrival(a, o):
        peer = lax.rem(seq + o, n_seq)
        src = (tokens, out_grad)[a]
        at = pl.ds(pl.multiple_of(peer * feats, feats), feats)
        return remote(src.at[:, at], cols_in.at[a, peer], a2a_send.at[a, peer],
                      a2a_recv.at[a, peer], "seq", peer)

    def start_a2a(o):
        for a in range(2):
            a2a(a, o).start()

    loop(1, n_seq, start_a2a)
    mine = pl.ds(pl.multiple_of(seq * feats, feats), feats)
    cols_in[0, seq] = tokens[:, mine]
    cols_in[1, seq] = out_grad[:, mine]
    total[...] = jnp.zeros_like(total)

    @pl.when(chip == 0)
    def _():
        left_got[...] = jnp.zeros_like(left_got)

    @pl.when(chip == last)
    def _():
        right_got[...] = jnp.zeros_like(right_got)

    def wait_a2a(o):
        for a in range(2):
            a2a_arrival(a, o).wait_recv()

    loop(1, n_seq, wait_a2a)
    for a in range(2):
        cols[a] = cols_in[a].astype(F32).reshape(n_tok, feats).astype(BF16)

    def core_copy(c):
        return remote(core_out.at[c], core_got.at[c], core_send.at[c],
                      core_recv.at[c], "seq", partner)

    def right_copy(c):
        return remote(right_out.at[c], left_got.at[c], right_send.at[c],
                      right_recv.at[c], "seq", right_dev)

    def left_copy(c):
        return remote(left_out.at[c], right_got.at[c], left_send.at[c],
                      left_recv.at[c], "seq", left_dev)

    def hid_copy(c, which):
        part = hidden.at[c, which]
        return remote(part, part, hid_send.at[c], hid_recv.at[c], "seq", partner)

    def step(i):
        @pl.when(i < n)
        def _():
            for copy in w_copies(i):
                copy.wait()
            pre = jnp.dot(cols[0], w_in_v[i], preferred_element_type=F32)
            grad = lax.dot_general(cols[1], w_out_v[i], (((1,), (1,)), ((), ())),
                                   preferred_element_type=F32)
            for a, value in enumerate((pre, grad)):
                low, high = value[:half], value[half:]
                own[i, a] = jnp.where(core == 0, low, high)
                core_out[i, a] = jnp.where(core == 0, high, low).astype(BF16)
            core_copy(i).start()

        near = i - CORE_LAG

        @pl.when((near >= 0) & (near < n))
        def _():
            core_copy(near).wait_recv()
            own[near] = own[near] + core_got[near].astype(F32)

        from_left = i - CORE_LAG - chip * LAG

        @pl.when((from_left >= 0) & (from_left < n))
        def _():
            @pl.when(chip > 0)
            def _():
                right_copy(from_left).wait_recv()

            @pl.when(chip < last)
            def _():
                right_out[from_left] = (
                    left_got[from_left].astype(F32) + own[from_left]
                ).astype(BF16)
                right_copy(from_left).start()

        from_right = i - CORE_LAG - (last - chip) * LAG

        @pl.when((from_right >= 0) & (from_right < n))
        def _():
            @pl.when(chip < last)
            def _():
                left_copy(from_right).wait_recv()

            @pl.when(chip > 0)
            def _():
                left_out[from_right] = (
                    right_got[from_right].astype(F32) + own[from_right]
                ).astype(BF16)
                left_copy(from_right).start()

        done = i - CORE_LAG - jnp.maximum(chip, last - chip) * LAG

        @pl.when((done >= 0) & (done < n))
        def _():
            value = own[done] + left_got[done].astype(F32) + right_got[done].astype(F32)
            posit = jnp.maximum(value[0], 0.0)
            hidden[done, core, 0] = (posit * posit).astype(BF16)
            hidden[done, core, 1] = (2.0 * posit * value[1]).astype(BF16)
            hid_copy(done, core).start()

        both = done - HID_LAG

        @pl.when((both >= 0) & (both < n))
        def _():
            hid_copy(both, 1 - core).wait_recv()
            slope = jnp.concatenate([hidden[both, 0, 1], hidden[both, 1, 1]], axis=0)
            part = lax.dot_general(slope, w_in_v[both], (((1,), (1,)), ((), ())),
                                   preferred_element_type=F32)
            total[...] += part.reshape(total.shape)

    loop(0, n + CORE_LAG + HID_LAG + last * LAG, step)

    def tp_copy(o):
        peer = lax.rem(tp + o, n_tp)
        return remote(total.at[peer], tp_got.at[tp], tp_send.at[peer],
                      tp_recv.at[tp], "tp", peer)

    def tp_arrival(o):
        peer = lax.rem(tp + o, n_tp)
        return remote(total.at[peer], tp_got.at[peer], tp_send.at[peer],
                      tp_recv.at[peer], "tp", peer)

    loop(1, n_tp, lambda o: tp_copy(o).start())
    outs = (
        pltpu.make_async_copy(hidden, hidden_out, out_sem.at[0]),
        pltpu.make_async_copy(cols, cols_out, out_sem.at[1]),
    )
    for copy in outs:
        copy.start()

    def wait_sends(c):
        core_copy(c).wait_send()
        hid_copy(c, core).wait_send()

        @pl.when(chip < last)
        def _():
            right_copy(c).wait_send()

        @pl.when(chip > 0)
        def _():
            left_copy(c).wait_send()

    loop(0, n, wait_sends)

    def wait_a2a_sends(o):
        for a in range(2):
            a2a(a, o).wait_send()

    loop(1, n_seq, wait_a2a_sends)
    loop(1, n_tp, lambda o: tp_arrival(o).wait_recv())
    tp_got[tp] = total[tp]
    input_grad[...] = jnp.sum(tp_got[...], axis=0).astype(BF16)
    loop(1, n_tp, lambda o: tp_copy(o).wait_send())
    for copy in outs:
        copy.wait()


def grads_kernel(hidden, cols, given, input_grad, grad_in, grad_out):
    input_grad[...] = given[...]
    act, slope = (
        jnp.concatenate(
            [
                jnp.concatenate([hidden[g, 0, a], hidden[g, 1, a]], axis=0)
                for g in range(hidden.shape[0])
            ],
            axis=1,
        )
        for a in range(2)
    )
    rows = (((0,), (0,)), ((), ()))
    grad_in[...] = lax.dot_general(cols[0], slope, rows, preferred_element_type=F32)
    grad_out[...] = lax.dot_general(act, cols[1], rows, preferred_element_type=F32)


def per_device(n_seq, n_tp, tokens, out_grad, w_in, w_out):
    n_tok = tokens.shape[0] * n_seq
    feats, units = w_in.shape
    wide = max(128, units // MOST_CHUNKS)
    half = n_tok // 2
    n = units // wide
    group = next(g for g in (4, 3, 2, 1) if n % g == 0)
    vmem = pl.BlockSpec(memory_space=pltpu.VMEM)
    hbm = pl.BlockSpec(memory_space=pl.ANY)
    dma = pltpu.SemaphoreType.DMA
    pair = (n, 2, half, wide)
    hidden, cols, input_grad = pl.pallas_call(
        functools.partial(hidden_kernel, n_seq, n_tp),
        out_shape=(
            jax.ShapeDtypeStruct((n, 2, 2, half, wide), BF16),
            jax.ShapeDtypeStruct((2, n_tok, feats), BF16),
            jax.ShapeDtypeStruct((n_tok // n_tp, feats), BF16),
        ),
        in_specs=[vmem, vmem, hbm, hbm],
        out_specs=(hbm, hbm, vmem),
        scratch_shapes=[
            pltpu.VMEM((n, feats, wide), BF16),
            pltpu.VMEM((n, wide, feats), BF16),
            pltpu.VMEM((2, n_seq, tokens.shape[0], feats), BF16),
            pltpu.VMEM((2, n_tok, feats), BF16),
            pltpu.VMEM(pair, F32),
            pltpu.VMEM(pair, BF16),
            pltpu.VMEM(pair, BF16),
            pltpu.VMEM(pair, BF16),
            pltpu.VMEM(pair, BF16),
            pltpu.VMEM(pair, BF16),
            pltpu.VMEM(pair, BF16),
            pltpu.VMEM((n, 2, 2, half, wide), BF16),
            pltpu.VMEM((n_tp, n_tok // n_tp, feats), F32),
            pltpu.VMEM((n_tp, n_tok // n_tp, feats), F32),
            dma((2, n)),
            dma((2, n_seq)),
            dma((2, n_seq)),
            dma((n,)),
            dma((n,)),
            dma((n,)),
            dma((n,)),
            dma((n,)),
            dma((n,)),
            dma((n,)),
            dma((n,)),
            dma((n_tp,)),
            dma((n_tp,)),
            dma((2,)),
        ],
        compiler_params=pltpu.CompilerParams(
            collective_id=0, has_side_effects=True, vmem_limit_bytes=56 * 1024 * 1024
        ),
        name="hidden_exchange",
    )(tokens, out_grad, w_in, w_out)

    whole = pl.BlockSpec((n_tok // n_tp, feats), lambda c: (0, 0))
    return pl.pallas_call(
        grads_kernel,
        grid=(n // group,),
        out_shape=(
            jax.ShapeDtypeStruct((n_tok // n_tp, feats), BF16),
            jax.ShapeDtypeStruct((feats, units), F32),
            jax.ShapeDtypeStruct((units, feats), F32),
        ),
        in_specs=[
            pl.BlockSpec((group, 2, 2, half, wide), lambda c: (c, 0, 0, 0, 0)),
            pl.BlockSpec((2, n_tok, feats), lambda c: (0, 0, 0)),
            whole,
        ],
        out_specs=(
            whole,
            pl.BlockSpec((feats, group * wide), lambda c: (0, c)),
            pl.BlockSpec((group * wide, feats), lambda c: (c, 0)),
        ),
        name="weight_grads",
    )(hidden, cols, input_grad)


def solution(mesh):
    return jax.shard_map(
        functools.partial(per_device, mesh.shape["seq"], mesh.shape["tp"]),
        mesh=mesh,
        in_specs=(P("seq", None), P("seq", None), P("seq", "tp"), P("tp", "seq")),
        out_specs=(P("tp", "seq"), P("seq", "tp"), P("tp", "seq")),
        check_vma=False,
    )
```
